32 devices in a mesh: img: 8 (over z, y), grp: 4 (over x, core).
Axes of the slice: x: 2, y: 2, z: 4, core: 2. Of those that a mesh axis runs over, the one named last changes fastest.
Arguments:
- images: bfloat16 [12288, 9216], P(('img', 'grp')), may hold values from -64 to 64, as said below
- expansion_basis: bfloat16 [9216, 960], P(None, 'img'), may hold values from -0.0625 to 0.0625
- block_sizes: int32 [16], replicated, may hold values from 1 to 80, 480 in all
- keep_count: int32 [16], replicated, may hold values from 1 to 8
- start_block: float32 [16, 80, 8], replicated, may hold values from -6 to 6
Outputs:
- features: float32 [12288, 256], P(('img', 'grp'))
- values: float32 [16, 8], replicated
The draws below stay inside these ranges and needn't reach their ends.
Inputs may be any that keep to these rules, and one draw needn't show every extreme that they name: `images`: pixel values of order one. `block_sizes`: the 16 sizes sum to 480.
All inputs are finite; a program needn't handle non-finite values.
Results may differ from the reference program's by a relative error of at most 0.025.
Values may be sent and summed in bfloat16 or wider, within the bound.
No kernel may reach another device: no remote copies, remote signals or barrier semaphores. Data moves between devices by JAX's collectives and lax.ppermute only.
A program may use at most 128 MiB of HBM per device.

```python
import math
import jax
import jax.numpy as jnp
import numpy as np
from jax import lax

PIX = 9216
NMAX = 80
L = 16
S = 480
KMAX = 8
ITERS = 3
P_SIZE = 384
NPART = 12288


def draw_images(key, part):
    first = jax.random.fold_in(key, 11)
    second = jax.random.fold_in(key, 23)
    third = jax.random.fold_in(key, 37)
    order = jnp.arange(NPART, dtype=jnp.float32) / max(NPART - 1, 1)
    row_scale = jnp.exp(jnp.log(3.0) * order) * jax.random.uniform(first, (NPART,), jnp.float32, 0.7, 1.4)
    column_scale = jnp.exp(jax.random.uniform(second, (PIX,), jnp.float32, jnp.log(0.3), jnp.log(3.0)))
    noise = jnp.clip(jax.random.normal(third, (NPART, PIX), jnp.float32), -5.0, 5.0)
    return (noise * row_scale[:, None] * column_scale[None, :]).astype(jnp.bfloat16)


def place_ends(values, key, low, top_value):
    extent = values.shape
    place = [jax.random.randint(jax.random.fold_in(key, axis), (), 0, extent[axis]) for axis in range(len(extent))]
    values = values.at[tuple(place)].set(low)
    longest = extent.index(max(extent))
    place[longest] = (place[longest] + 1) % extent[longest]
    return values.at[tuple(place)].set(top_value)


def level_of(key, dims, shards, low, high):
    def one(position, parts):
        heights = jax.random.uniform(jax.random.fold_in(jax.random.fold_in(key, 6), position), (parts,), jnp.float32, low / len(shards), high / len(shards))
        return jnp.repeat(jnp.exp(heights), dims[position] // parts).reshape((-1,) + (1,) * (len(dims) - position - 1))

    gain = one(*shards[0])
    for cut in shards[1:]:
        gain = gain * one(*cut)
    return gain


def split_up(count, total, most, skew):
    loads = [(1 << 20) // math.isqrt(grade ** skew) + 1 for grade in range(2, count + 1)]
    surplus, given = total - most - (count - 1), [1] * (count - 1)
    while surplus > 0:
        movable = [i for i in range(count - 1) if given[i] < most]
        whole, budget = sum([loads[i] for i in movable]), surplus
        for i in movable:
            addition = min(most - given[i], max(1, budget * loads[i] // whole), surplus)
            given[i] = given[i] + addition
            surplus = surplus - addition
    return np.array([most] + given)


def ragged(rng, number_of, total, bound, slope):
    if number_of == 2:
        one = jax.random.randint(rng, (), max(1, total - bound), min(bound, total - 1) + 1)
        return jnp.stack([one, total - one])
    lengths = jnp.asarray(split_up(number_of, total, bound, slope), jnp.int32)
    pairs = (number_of - 1) // 2
    donor, sink = lengths[1:1 + 2 * pairs:2], lengths[2:2 + 2 * pairs:2]
    margin = jnp.minimum(donor - 1, bound - sink)
    moved = jax.random.randint(jax.random.fold_in(rng, 1), (pairs,), 0, 1 << 20) % (margin + 1)
    lengths = lengths.at[1:1 + 2 * pairs:2].set(donor - moved).at[2:2 + 2 * pairs:2].set(sink + moved)
    return lengths[jax.random.permutation(jax.random.fold_in(rng, 2), number_of)]


def bell_draw(rng, dims, spread, bound, pieces=(), held_as=jnp.bfloat16):
    drawn = spread * jax.random.normal(rng, dims, jnp.float32)
    if pieces:
        drawn = drawn * level_of(rng, dims, pieces, -0.22, 0.18)
    return jnp.clip(drawn, -bound, bound).astype(held_as)


def setup_inputs(seed: int = 0) -> dict:
    key_list = jax.random.split(jax.random.key(seed), 6)
    images = draw_images(jax.random.fold_in(key_list[5], 71), 0)
    expansion_basis = bell_draw(key_list[1], (PIX, 2 * S), PIX ** -0.5, 0.0625, ((1, 8),))
    block_sizes = ragged(key_list[2], L, S, NMAX, 2).astype(jnp.int32)
    keep_count = place_ends(jax.random.randint(key_list[3], (L,), 1, KMAX + 1), jax.random.fold_in(key_list[3], 1), 1, KMAX).astype(jnp.int32)
    start_block = bell_draw(key_list[4], (L, NMAX, KMAX), 1.0, 6.0, (), jnp.float32)
    return dict(images=images, expansion_basis=expansion_basis, block_sizes=block_sizes, keep_count=keep_count, start_block=start_block)


HIGH = lax.Precision.HIGHEST

def selector(block_sizes, total, count, width):
    offsets = jnp.cumsum(block_sizes) - block_sizes
    column = jnp.arange(total, dtype=jnp.int32)[:, None, None]
    inside = jnp.arange(width, dtype=jnp.int32)[None, None, :]
    hit = (column == offsets[None, :, None] + inside) & (inside < block_sizes[None, :, None])
    return hit.astype(jnp.bfloat16).reshape(total, count * width)

def subspace(cover, block_sizes, keep_count, start_block):
    width = cover.shape[1]
    ranks = start_block.shape[2]
    inside = jnp.arange(width, dtype=jnp.int32)[None, :, None] < block_sizes[:, None, None]
    keep = jnp.minimum(keep_count, (block_sizes + 1) // 2)
    current = jnp.where(inside, start_block, jnp.zeros_like(start_block))
    for turn in range(ITERS):
        product = jnp.einsum('bij,bjk->bik', cover, current, precision=HIGH)
        columns = []
        for column_id in range(ranks):
            vector = product[:, :, column_id]
            for earlier in columns:
                vector = vector - lax.optimization_barrier(jnp.sum(earlier * vector, axis=1, keepdims=True)) * earlier
            length = jnp.sqrt(lax.optimization_barrier(jnp.sum(vector * vector, axis=1, keepdims=True)))
            alive = (column_id < keep)[:, None]
            columns.append(jnp.where(alive, vector / length, jnp.zeros_like(vector)))
        current = jnp.stack(columns, axis=2)
    product = jnp.einsum('bij,bjk->bik', cover, current, precision=HIGH)
    found = lax.optimization_barrier(jnp.sum(current * product, axis=1))
    return (current, found)

def reference(images, expansion_basis, block_sizes, keep_count, start_block):
    count_all = images.shape[0] // P_SIZE
    pick = selector(block_sizes, S, L, NMAX)
    scale = 1.0 / (2 * images.shape[0])

    def accumulate(total, span_rows):
        coeffs = jnp.dot(span_rows, expansion_basis, preferred_element_type=jnp.float32).astype(jnp.bfloat16)
        samples = coeffs.reshape(2 * P_SIZE, S)
        padded = jnp.dot(samples, pick, preferred_element_type=jnp.float32).astype(jnp.bfloat16)
        wide = padded.astype(jnp.float32).reshape(2 * P_SIZE, L, NMAX)
        partial_value = jnp.einsum('rli,rlj->lij', wide, wide, precision=HIGH) * scale
        return (total + partial_value, padded)
    start_total = jnp.zeros((L, NMAX, NMAX), jnp.float32)
    cover, padded_all = lax.scan(accumulate, start_total, images.reshape(count_all, P_SIZE, PIX))
    vectors, found = subspace(cover, block_sizes, keep_count, start_block)
    rounded = vectors.astype(jnp.bfloat16).astype(jnp.float32)
    wide_all = padded_all.reshape(count_all * 2 * P_SIZE, L, NMAX).astype(jnp.float32)
    features = jnp.einsum('rli,lij->rlj', wide_all, rounded, precision=HIGH)
    return (features.reshape(images.shape[0], 2 * L * KMAX), found)
```

```python
import jax
import jax.numpy as jnp
from jax import lax
from jax.experimental import pallas as pl
from jax.experimental.pallas import tpu as pltpu
from jax.sharding import PartitionSpec as P

NMAX = 80
L = 16
S = 480
KMAX = 8
ITERS = 3
LANES = 128
WIDE = -(-S // LANES) * LANES
TALL = WIDE + NMAX
AXES = ("img", "grp")
HIGH = lax.Precision.HIGHEST


def gram_kernel(offs, sizes, coeffs_ref, out_ref, gram, packed, *, scale):
    total = None
    for part in range(2):
        rows = coeffs_ref[:, part * WIDE : (part + 1) * WIDE]
        one = lax.dot_general(
            rows, rows, (((0,), (0,)), ((), ())), preferred_element_type=jnp.float32
        )
        total = one if total is None else total + one
    gram[...] = jnp.zeros_like(gram)
    for tile in range(WIDE // LANES):
        gram[tile, :WIDE, :] = total[:, tile * LANES : (tile + 1) * LANES] * scale
    packed[...] = jnp.zeros_like(packed)
    lane = lax.broadcasted_iota(jnp.int32, (NMAX, LANES), 1)
    for l in range(L):
        off = offs[l]
        tile = off // LANES
        turn = LANES - off % LANES
        left = pltpu.roll(gram[tile, pl.ds(off, NMAX), :], turn % LANES, 1)
        right = pltpu.roll(gram[tile + 1, pl.ds(off, NMAX), :], turn % LANES, 1)
        block = jnp.where(lane < turn, left, right)
        packed[pl.ds(off, NMAX), :] = jnp.where(lane < sizes[l], block, 0.0)
    out_ref[...] = packed[:WIDE, :]


def packed_cover(coeffs, offs, sizes, scale):
    return pl.pallas_call(
        lambda *refs: gram_kernel(*refs, scale=scale),
        grid_spec=pltpu.PrefetchScalarGridSpec(
            num_scalar_prefetch=2,
            grid=(),
            in_specs=[pl.BlockSpec(memory_space=pltpu.VMEM)],
            out_specs=pl.BlockSpec(memory_space=pltpu.VMEM),
            scratch_shapes=[
                pltpu.VMEM((WIDE // LANES + 1, TALL, LANES), jnp.float32),
                pltpu.VMEM((TALL, LANES), jnp.float32),
            ],
        ),
        out_shape=jax.ShapeDtypeStruct((WIDE, LANES), jnp.float32),
        name="gram",
    )(offs, sizes, coeffs)


def solve_kernel(places, offs, sizes, lanes_ref, start_ref, coeffs_ref, *refs, blocks):
    cover_refs = refs[:blocks]
    out_ref, values_ref, packed, cover, spread = refs[blocks:]
    packed[...] = jnp.zeros_like(packed)
    for b, ref in enumerate(cover_refs):
        size = ref.shape[0]
        packed[pl.ds(pl.multiple_of(places[b], 8), size), :] = ref[...]
    row = lax.broadcasted_iota(jnp.int32, (NMAX, LANES), 0)
    lane = lax.broadcasted_iota(jnp.int32, (NMAX, LANES), 1)
    group = lane // KMAX
    column = lane % KMAX
    for l in range(L):
        block = packed[pl.ds(offs[l], NMAX), :]
        cover[l * NMAX : (l + 1) * NMAX, :] = jnp.where(row < sizes[l], block, 0.0)
    size_lane = lanes_ref[0:1, :]
    keep_lane = lanes_ref[1:2, :]

    def product(current):
        tall = jnp.concatenate(
            [current, jnp.zeros((LANES - NMAX, LANES), jnp.float32)], axis=0
        )
        result = jnp.dot(
            cover[...], tall, precision=HIGH, preferred_element_type=jnp.float32
        )
        total = jnp.zeros((NMAX, LANES), jnp.float32)
        for l in range(L):
            total = jnp.where(group == l, result[l * NMAX : (l + 1) * NMAX, :], total)
        return total

    current = jnp.where(row < size_lane, start_ref[...], 0.0)
    for turn in range(ITERS):
        current = product(current)
        for m in range(KMAX):
            own = jnp.take_along_axis(current, group * KMAX + m, axis=1)
            inner = jnp.sum(own * current, axis=0, keepdims=True)
            square = jnp.sum(own * own, axis=0, keepdims=True)
            scale = 1.0 / jnp.sqrt(square)
            alive = keep_lane > m
            unit = jnp.where(alive, own * scale, 0.0)
            along = jnp.where(alive, inner * scale, 0.0)
            current = jnp.where(
                column == m,
                unit,
                jnp.where(column > m, current - along * unit, current),
            )
    values_ref[...] = jnp.sum(current * product(current), axis=0, keepdims=True)
    spread[...] = jnp.zeros_like(spread)
    for l in range(L):
        spread[pl.ds(offs[l], NMAX), :] = jnp.where(group == l, current, 0.0)
    rounded = spread[:WIDE, :].astype(jnp.bfloat16)
    for part in range(2):
        out_ref[:, part * LANES : (part + 1) * LANES] = jnp.dot(
            coeffs_ref[:, part * WIDE : (part + 1) * WIDE],
            rounded,
            preferred_element_type=jnp.float32,
        )


def solve(pieces, places, coeffs, offs, sizes, keep_count, start_block):
    keep = jnp.minimum(keep_count, (sizes + 1) // 2)
    per_lane = jnp.stack([jnp.repeat(sizes, KMAX), jnp.repeat(keep, KMAX)])
    start = start_block.transpose(1, 0, 2).reshape(NMAX, L * KMAX)
    rows = coeffs.shape[0]
    vmem = pl.BlockSpec(memory_space=pltpu.VMEM)
    features, values = pl.pallas_call(
        lambda *refs: solve_kernel(*refs, blocks=len(pieces)),
        grid_spec=pltpu.PrefetchScalarGridSpec(
            num_scalar_prefetch=3,
            grid=(),
            in_specs=[vmem] * (3 + len(pieces)),
            out_specs=[vmem, vmem],
            scratch_shapes=[
                pltpu.VMEM((TALL, LANES), jnp.float32),
                pltpu.VMEM((L * NMAX, LANES), jnp.float32),
                pltpu.VMEM((TALL, LANES), jnp.float32),
            ],
        ),
        out_shape=[
            jax.ShapeDtypeStruct((rows, 2 * LANES), jnp.float32),
            jax.ShapeDtypeStruct((1, LANES), jnp.float32),
        ],
        name="solve",
    )(places, offs, sizes, per_lane, start, coeffs, *pieces)
    return features, values.reshape(L, KMAX)


class Grid:
    def __init__(self, n_img, n_grp):
        self.n_img, self.n_grp = n_img, n_grp
        img, grp = lax.axis_index("img"), lax.axis_index("grp")
        self.z, self.y, self.x, self.c = img // 2, img % 2, grp // 2, grp % 2

    def pairs(self, move):
        found = []
        for d in range(self.n_img * self.n_grp):
            img, grp = divmod(d, self.n_grp)
            here = (img // 2, img % 2, grp // 2, grp % 2)
            there = move(*here)
            if there is not None:
                z, y, x, c = there
                found.append((d, (z * 2 + y) * self.n_grp + x * 2 + c))
        return found

    def send(self, value, move):
        return lax.ppermute(value, AXES, self.pairs(move))


def reduce_pieces(grid, cover):
    c, q = grid.c, grid.x * 2 + grid.y
    half = cover.shape[0] // 2
    part = half // 4
    cut = lax.dynamic_slice_in_dim
    flip = lambda z, y, x, c: (z, y, x, 1 - c)
    held = cut(cover, c * half, half) + grid.send(cut(cover, (1 - c) * half, half), flip)
    turns = []
    for e in (1, 2, 3):
        turns.append(lambda z, y, x, c, e=e: (z, y ^ (e & 1), x ^ (e >> 1), c))
    got = [grid.send(cut(held, (q ^ e) * part, part), turns[e - 1]) for e in (1, 2, 3)]
    mine = (cut(held, q * part, part) + got[0]) + (got[1] + got[2])
    far = [
        grid.send(mine, lambda z, y, x, c, e=e: (z ^ e, y, x, c)) for e in (1, 2, 3)
    ]
    mine = (mine + far[0]) + (far[1] + far[2])
    twin = grid.send(mine, flip)
    both = jnp.concatenate([mine, twin], axis=0)
    pieces = [mine, twin]
    places = [c * half + q * part, (1 - c) * half + q * part]
    for e in (1, 2, 3):
        other = grid.send(both, turns[e - 1])
        pieces += [other[:part], other[part:]]
        places += [c * half + (q ^ e) * part, (1 - c) * half + (q ^ e) * part]
    return pieces, jnp.stack(places)


def gathered_coeffs(grid, images, basis):
    z, y, x, c = grid.z, grid.y, grid.x, grid.c
    pixels, width = basis.shape
    rows = images.shape[0]
    quarter = pixels // 4
    cut = lax.dynamic_slice_in_dim
    send = grid.send
    at = lambda core, side: (core * 2 + side) * quarter
    flip = lambda z, y, x, c: (z, y, x, 1 - c)
    over_y = lambda z, y, x, c: (z, 1 - y, x, c)
    over_x = lambda z, y, x, c: (z, y, 1 - x, c)
    near = lambda z, y, x, c: (z ^ 1, y, x, c)
    middle = lambda z, y, x, c: (3 - z, y, x, c) if z in (1, 2) else None
    outward = lambda z, y, x, c: (z ^ 1, y, x, c) if z in (1, 2) else None
    is_middle = (z == 1) | (z == 2)

    own_a = cut(basis, at(c, x), quarter)
    own_b = cut(basis, at(c, 1 - x), quarter)
    near_a = send(own_a, near)
    mid_c_a = send(own_a, middle)
    y_own_a = send(own_a, over_y)
    pix_a = jnp.concatenate(
        [cut(images, at(c, x), quarter, 1), send(cut(images, at(1 - c, x), quarter, 1), flip)], 0
    )
    pix_b = jnp.concatenate(
        [cut(images, at(c, 1 - x), quarter, 1), send(cut(images, at(1 - c, 1 - x), quarter, 1), flip)], 0
    )
    far_c_a = jnp.where(is_middle, mid_c_a, send(mid_c_a, outward))
    mid_d_a = send(near_a, middle)
    y_near_a = send(near_a, over_y)
    near_b = send(near_a, over_x)
    mid_c_b = send(own_b, middle)
    far_d_a = jnp.where(is_middle, mid_d_a, send(mid_d_a, outward))
    y_c_a = send(far_c_a, over_y)
    y_near_b = send(y_near_a, over_x)
    mid_d_b = send(near_b, middle)
    far_c_b = jnp.where(is_middle, mid_c_b, send(mid_c_b, outward))
    y_d_a = send(far_d_a, over_y)
    y_c_b = send(y_c_a, over_x)
    far_d_b = jnp.where(is_middle, mid_d_b, send(mid_d_b, outward))
    y_own_b = send(own_b, over_y)
    y_d_b = send(y_d_a, over_x)

    def times(a, b):
        total = jnp.dot(pix_a, a, preferred_element_type=jnp.float32)
        total = total + jnp.dot(pix_b, b, preferred_element_type=jnp.float32)
        return total[:rows] + send(total[rows:], flip)

    own = [times(own_a, own_b), times(near_a, near_b), times(far_c_a, far_c_b), times(far_d_a, far_d_b)]
    mate = [times(y_own_a, y_own_b), times(y_near_a, y_near_b), times(y_c_a, y_c_b), times(y_d_a, y_d_b)]
    low = z < 2
    parts = [[], []]
    for at_z in range(4):
        for at_y in range(2):
            pick = [jnp.where(y == at_y, a, b) for a, b in zip(own, mate)]
            if at_z in (0, 1):
                far = pick[3 - at_z]
                value = jnp.where(low, jnp.where(z == at_z, pick[0], pick[1]), far)
            else:
                far = pick[at_z]
                value = jnp.where(low, far, jnp.where(z == at_z, pick[0], pick[1]))
            parts[at_z // 2].append(value.astype(jnp.bfloat16))
    blank = jnp.zeros((rows, WIDE - S), jnp.bfloat16)
    return jnp.concatenate(parts[0] + [blank] + parts[1] + [blank], axis=1)


def padded_coeffs(images, basis):
    whole = lax.all_gather(basis, "img", axis=1, tiled=True)
    coeffs = jnp.dot(images, whole, preferred_element_type=jnp.float32).astype(jnp.bfloat16)
    rows = images.shape[0]
    return jnp.pad(coeffs.reshape(rows, 2, S), ((0, 0), (0, 0), (0, WIDE - S))).reshape(rows, 2 * WIDE)


def per_device(images, expansion_basis, block_sizes, keep_count, start_block):
    n_img, n_grp = lax.axis_size("img"), lax.axis_size("grp")
    rows = images.shape[0]
    offs = jnp.cumsum(block_sizes) - block_sizes
    scale = 1.0 / (2 * rows * n_img * n_grp)
    direct = (n_img, n_grp) == (8, 4)
    if direct:
        grid = Grid(n_img, n_grp)
        coeffs = gathered_coeffs(grid, images, expansion_basis)
    else:
        coeffs = padded_coeffs(images, expansion_basis)
    cover = packed_cover(coeffs, offs, block_sizes, scale)
    if direct:
        pieces, places = reduce_pieces(grid, cover)
    else:
        pieces, places = [lax.psum(cover, AXES)], jnp.zeros((1,), jnp.int32)
    return solve(pieces, places, coeffs, offs, block_sizes, keep_count, start_block)


def solution(mesh):
    in_specs = (P(AXES, None), P(None, "img"), P(), P(), P())
    out_specs = (P(AXES, None), P())
    return jax.shard_map(
        per_device, mesh=mesh, in_specs=in_specs, out_specs=out_specs, check_vma=False
    )
```
